32 devices in a mesh: row: 8 (over y, x, core), col: 4 (over z).
Axes of the slice: x: 2, y: 2, z: 4, core: 2. Of those that a mesh axis runs over, the one named last changes fastest.
Arguments:
- sequence: bfloat16 [32768, 1536], P(('row', 'col')), may hold values from -6 to 6
- filter_weight: bfloat16 [3, 1536, 1536], replicated, may hold values from -0.09375 to 0.09375
- pair_proj: bfloat16 [1536, 256], replicated, may hold values from -0.15625 to 0.15625
- pair_out: bfloat16 [128, 128], replicated, may hold values from -0.5 to 0.5
- donor_w: bfloat16 [1536, 128], replicated, may hold values from -0.15625 to 0.15625
- donor_pos: int32 [8192], P(('row', 'col')), may hold values from 0 to 1023
- acceptor_bin: int32 [8192], P(('row', 'col')), may hold values from 0 to 255, as said below
Outputs:
- pair: bfloat16 [256, 256, 128], P('row', 'col')
- junctions: bfloat16 [8192, 128], P(('row', 'col'))
The draws below stay inside these ranges and needn't reach their ends.
Inputs may be any that keep to these rules, and one draw needn't show every extreme that they name: Among the 256 junctions of one device at most 64 have acceptor_bin in any one block of 64 pair columns; on every device some block holds exactly 64.
All inputs are finite; a program needn't handle non-finite values.
Results may differ from the reference program's by a relative error of at most 0.013.
Values may be sent and summed in bfloat16 or wider, within the bound.
A program may use at most 128 MiB of HBM per device.

```python
import jax
import jax.numpy as jnp
from jax import lax

D = 1536
PCH = 128
ROWS_DEV = 1024
DILATION_STEP = 32
POOL = 128
JUNC_DEV = 256
CAP = 64
SEQ = 32768
P_SIZE = 256
PC = 64
SLOTS = 256
NJ = 8192
JROWS = 8192
N_COL = 4
DEVICES = 32


def draw_acceptor_bin(key, part):
    slot_total_count = N_COL * CAP
    key_hot, key_forced, key_jitter, key_within = jax.random.split(key, 4)
    hotness_level = jax.random.randint(key_hot, (N_COL,), 0, 4)
    forced_choice = jax.random.randint(key_forced, (DEVICES,), 0, N_COL)
    random_noise = jax.random.randint(key_jitter, (DEVICES, slot_total_count), 0, 4096)
    group_labels = jnp.arange(slot_total_count, dtype=jnp.int32) // CAP
    extra_score = jnp.where(group_labels[None, :] == forced_choice[:, None], 1 << 20, 0)
    score_values = (random_noise + hotness_level[group_labels][None, :] * 4096 + extra_score) * slot_total_count + jnp.arange(slot_total_count, dtype=jnp.int32)[None, :]
    _, chosen = lax.top_k(score_values, JUNC_DEV)
    chosen_group = chosen // CAP
    within = jax.random.randint(key_within, (DEVICES, JUNC_DEV), 0, PC)
    return (chosen_group * PC + within).reshape(-1).astype(jnp.int32)


def with_ends(drawn, key, smallest, largest):
    shape = drawn.shape
    place = [jax.random.randint(jax.random.fold_in(key, axis), (), 0, shape[axis]) for axis in range(len(shape))]
    drawn = drawn.at[tuple(place)].set(smallest)
    longest = shape.index(max(shape))
    place[longest] = (place[longest] + 1) % shape[longest]
    return drawn.at[tuple(place)].set(largest)


def block_scale(stream_key, extent, cuts, least, top_value):
    def one(position, parts):
        steps = jax.random.uniform(jax.random.fold_in(jax.random.fold_in(stream_key, 6), position), (parts,), jnp.float32, least / len(cuts), top_value / len(cuts))
        return jnp.repeat(jnp.exp(steps), extent[position] // parts).reshape((-1,) + (1,) * (len(extent) - position - 1))

    factor_of = one(*cuts[0])
    for cut in cuts[1:]:
        factor_of = factor_of * one(*cut)
    return factor_of


def scatter_about(key, shape, scale, limit, cuts=(), kind=jnp.bfloat16):
    values = jax.random.normal(key, shape, jnp.float32) * scale
    if len(cuts) > 0:
        values = block_scale(key, shape, cuts, -0.22, 0.18) * values
    return jnp.clip(values, min=-limit, max=limit).astype(kind)


def setup_inputs(seed: int = 0) -> dict:
    keys = jax.random.split(jax.random.key(seed), 8)
    return {
        "sequence": scatter_about(keys[0], (SEQ, D), 1.0, 6.0, ((0, 32),)),
        "filter_weight": scatter_about(keys[1], (3, D, D), (3 * D) ** -0.5, 0.09375),
        "pair_proj": scatter_about(keys[2], (D, 2 * PCH), D ** -0.5, 0.15625),
        "pair_out": scatter_about(keys[3], (PCH, PCH), PCH ** -0.5, 0.5),
        "donor_w": scatter_about(keys[4], (D, PCH), D ** -0.5, 0.15625),
        "donor_pos": with_ends(jax.random.randint(keys[5], (NJ,), 0, ROWS_DEV), jax.random.fold_in(keys[5], 1), 0, ROWS_DEV - 1).astype(jnp.int32),
        "acceptor_bin": draw_acceptor_bin(jax.random.fold_in(keys[7], 71), 0),
    }


def reference(sequence, filter_weight, pair_proj, pair_out, donor_w, donor_pos, acceptor_bin):
    sequence_length = sequence.shape[0]
    padded_sequence = jnp.pad(sequence, ((DILATION_STEP, DILATION_STEP), (0, 0)))
    filtered_rows = jnp.dot(padded_sequence[0:sequence_length], filter_weight[0], preferred_element_type=jnp.float32)
    filtered_rows = filtered_rows + jnp.dot(padded_sequence[DILATION_STEP:DILATION_STEP + sequence_length], filter_weight[1], preferred_element_type=jnp.float32)
    filtered_rows = filtered_rows + jnp.dot(padded_sequence[2 * DILATION_STEP:2 * DILATION_STEP + sequence_length], filter_weight[2], preferred_element_type=jnp.float32)
    hidden = (sequence.astype(jnp.float32) + jax.nn.silu(filtered_rows)).astype(jnp.bfloat16)
    pooled = hidden.reshape(P_SIZE, POOL, D).astype(jnp.float32).mean(axis=1)
    normed = (pooled * lax.rsqrt(lax.optimization_barrier(jnp.mean(pooled * pooled, axis=-1, keepdims=True)) + 1e-06)).astype(jnp.bfloat16)
    projected = jnp.dot(normed, pair_proj, preferred_element_type=jnp.float32).astype(jnp.bfloat16)
    row_side = projected[:, :PCH].astype(jnp.float32)
    col_side = projected[:, PCH:].astype(jnp.float32)
    pair_hidden = jax.nn.relu(row_side[:, None, :] + col_side[None, :, :]).astype(jnp.bfloat16)
    pair = jnp.dot(pair_hidden.reshape(P_SIZE * P_SIZE, PCH), pair_out, preferred_element_type=jnp.float32)
    pair = pair.astype(jnp.bfloat16).reshape(P_SIZE, P_SIZE, PCH)
    sender = (jnp.arange(NJ) // JUNC_DEV).astype(jnp.int32)
    global_pos = (sender * ROWS_DEV + donor_pos).astype(jnp.int32)
    donor_rows = hidden[global_pos]
    donor_emb = jnp.dot(donor_rows, donor_w, preferred_element_type=jnp.float32).astype(jnp.bfloat16)
    looked = pair[global_pos // POOL, acceptor_bin]
    junction_value = jax.nn.relu(donor_emb.astype(jnp.float32) + looked.astype(jnp.float32)).astype(jnp.bfloat16)
    col_group = (acceptor_bin // PC).astype(jnp.int32)
    onehot = (col_group.reshape(DEVICES, JUNC_DEV)[:, :, None] == jnp.arange(N_COL, dtype=jnp.int32)[None, None, :]).astype(jnp.int32)
    earlier = jnp.cumsum(onehot, axis=1) - onehot
    slot_rank = lax.optimization_barrier(jnp.sum(earlier * onehot, axis=-1)).reshape(NJ).astype(jnp.int32)
    owner_index = sender // N_COL * N_COL + col_group
    target_row = (owner_index * SLOTS + sender % N_COL * CAP + slot_rank).astype(jnp.int32)
    junctions = jnp.zeros((JROWS, PCH), jnp.bfloat16).at[target_row].set(junction_value)
    return (pair, junctions)
```

```python
import functools

import jax
import jax.numpy as jnp
from jax import lax
from jax.experimental import pallas as pl
from jax.experimental.pallas import tpu as pltpu
from jax.sharding import PartitionSpec as P

DILATION_STEP = 32
POOL = 128
CAP = 64
LANES = 128
CHUNK = 256
PRE = 3
MESH = pl.DeviceIdType.MESH
F32 = jnp.float32
BF16 = jnp.bfloat16


def dot(a, b):
    return jnp.dot(a, b, preferred_element_type=F32)


def trunk(
    n_row,
    n_col,
    x_hbm,
    w_hbm,
    proj_ref,
    donor_ref,
    pos_ref,
    bin_ref,
    rows_out,
    cols_out,
    emb_out,
    coord_out,
    xbuf,
    wbuf,
    early,
    emb_acc,
    pooled,
    select,
    row_send,
    col_send,
    emb_send,
    coord_send,
    x_sem,
    w_sem,
    halo_send_sem,
    halo_recv_sem,
    coord_send_sem,
    coord_recv_sem,
    emb_send_sem,
    emb_recv_sem,
    row_send_sem,
    row_recv_sem,
    col_send_sem,
    col_recv_sem,
):
    rows, width = x_hbm.shape
    halo = DILATION_STEP
    chunks = width // CHUNK
    pre = min(PRE, chunks)
    bins = rows // POOL
    tile_cols = bins * n_row
    slots = n_col * CAP
    count = n_row * n_col
    my_row = lax.axis_index("row")
    my_col = lax.axis_index("col")
    me = my_row * n_col + my_col

    def place(flat):
        return (flat // n_col, lax.rem(flat, n_col))

    def w_copy(tap, n):
        return pltpu.make_async_copy(
            w_hbm.at[tap, :, pl.ds(pl.multiple_of(n * CHUNK, CHUNK), CHUNK)], wbuf.at[n, tap], w_sem.at[n, tap]
        )

    x_copy = pltpu.make_async_copy(x_hbm, xbuf.at[pl.ds(halo, rows)], x_sem)
    w_copy(1, 0).start()
    x_copy.start()
    for n in range(1, pre):
        w_copy(1, n).start()
    for n in range(chunks):
        w_copy(0, n).start()
        w_copy(2, n).start()
        if n + pre < chunks:
            w_copy(1, n + pre).start()

    has_left = me > 0
    has_right = me < count - 1
    col_home = me // n_row
    self_col = col_home == my_col
    barrier = pltpu.get_barrier_semaphore()

    @pl.when(has_left)
    def _():
        pl.semaphore_signal(barrier, inc=1, device_id=place(me - 1), device_id_type=MESH)

    @pl.when(has_right)
    def _():
        pl.semaphore_signal(barrier, inc=1, device_id=place(me + 1), device_id_type=MESH)

    for d in range(1, n_col):
        pl.semaphore_signal(barrier, inc=1, device_id=(my_row, lax.rem(my_col + d, n_col)), device_id_type=MESH)
    for i in range(n_row):
        source = my_col * n_row + i

        @pl.when(source != me)
        def _():
            pl.semaphore_signal(barrier, inc=1, device_id=place(source), device_id_type=MESH)

    pos = pos_ref[...]
    acceptor = bin_ref[...]
    listed = pos.shape[1]
    group = jnp.zeros_like(acceptor)
    for k in range(1, n_col):
        group = group + jnp.where(acceptor >= k * tile_cols, 1, 0)
    pair_col = acceptor - group * tile_cols
    kinds = max(16, n_col)
    in_group = lax.broadcasted_iota(jnp.int32, (kinds, listed), 0) == group
    before = lax.broadcasted_iota(jnp.int32, (listed, listed), 0) < lax.broadcasted_iota(jnp.int32, (listed, listed), 1)
    in_group = jnp.where(in_group, 1.0, 0.0)
    earlier = dot(in_group.astype(BF16), jnp.where(before, 1.0, 0.0).astype(BF16))
    rank = jnp.sum(in_group * earlier, axis=0, keepdims=True)
    slot = group.astype(F32) * float(CAP) + rank
    slot_hot = lax.broadcasted_iota(jnp.int32, (slots, listed), 0).astype(F32) == slot
    slot_hot = jnp.where(slot_hot, 1.0, 0.0).astype(BF16)

    def spread(hot):
        return lax.dot_general(
            slot_hot, jnp.where(hot, 1.0, 0.0).astype(BF16), (((1,), (1,)), ((), ())), preferred_element_type=F32
        ).astype(BF16)

    col_lanes = coord_send.shape[2] - LANES
    col_hot = lax.broadcasted_iota(jnp.int32, (col_lanes, listed), 0) == pair_col
    coord_send[:, :, :col_lanes] = spread(col_hot).reshape(n_col, CAP, col_lanes)
    base = lax.broadcasted_iota(jnp.int32, (LANES, listed), 0) * POOL
    row_hot = (pos >= base) & (pos < base + POOL)
    coord_send[:, :, col_lanes:] = spread(row_hot).reshape(n_col, CAP, LANES)
    select[...] = spread(lax.broadcasted_iota(jnp.int32, (rows, listed), 0) == pos)

    neighbours = jnp.where(has_left, 1, 0) + jnp.where(has_right, 1, 0)
    pl.semaphore_wait(barrier, neighbours + n_col - 1 + n_row - jnp.where(self_col, 1, 0))

    def up_copy():
        return pltpu.make_async_remote_copy(
            src_ref=x_hbm.at[pl.ds(0, halo)],
            dst_ref=xbuf.at[pl.ds(rows + halo, halo)],
            send_sem=halo_send_sem.at[0],
            recv_sem=halo_recv_sem.at[0],
            device_id=place(me - 1),
            device_id_type=MESH,
        )

    def down_copy():
        return pltpu.make_async_remote_copy(
            src_ref=x_hbm.at[pl.ds(rows - halo, halo)],
            dst_ref=xbuf.at[pl.ds(0, halo)],
            send_sem=halo_send_sem.at[1],
            recv_sem=halo_recv_sem.at[1],
            device_id=place(me + 1),
            device_id_type=MESH,
        )

    def row_group_copies(src, dst, send_sem, recv_sem, whole):
        copies = []
        for d in range(1, n_col):
            there = lax.rem(my_col + d, n_col)
            copies.append(
                pltpu.make_async_remote_copy(
                    src_ref=src if whole else src.at[there],
                    dst_ref=dst.at[my_col],
                    send_sem=send_sem.at[d - 1],
                    recv_sem=recv_sem.at[d - 1],
                    device_id=(my_row, there),
                    device_id_type=MESH,
                )
            )
        return copies

    def row_group_arrivals(src, dst, send_sem, recv_sem):
        for d in range(1, n_col):
            source = lax.rem(my_col + n_col - d, n_col)
            pltpu.make_async_remote_copy(
                src_ref=src,
                dst_ref=dst.at[source],
                send_sem=send_sem.at[d - 1],
                recv_sem=recv_sem.at[d - 1],
                device_id=(my_row, source),
                device_id_type=MESH,
            ).wait_recv()

    @pl.when(has_left)
    def _():
        up_copy().start()

    @pl.when(has_right)
    def _():
        down_copy().start()

    coord_copies = row_group_copies(coord_send, coord_out, coord_send_sem, coord_recv_sem, False)
    for copy in coord_copies:
        copy.start()
    coord_out[my_col] = coord_send[my_col]

    @pl.when(jnp.logical_not(has_left))
    def _():
        xbuf[0:halo] = jnp.zeros((halo, width), BF16)

    @pl.when(jnp.logical_not(has_right))
    def _():
        xbuf[rows + halo : rows + 2 * halo] = jnp.zeros((halo, width), BF16)

    x_copy.wait()

    def centre(n, carry):
        w_copy(1, n).wait()
        early[n] = dot(xbuf[halo : halo + rows], wbuf[n, 1])
        return carry

    lax.fori_loop(0, pre, centre, 0)

    @pl.when(has_left)
    def _():
        down = down_copy()
        down.wait_recv()

    @pl.when(has_right)
    def _():
        up = up_copy()
        up.wait_recv()

    emb_acc[...] = jnp.zeros_like(emb_acc)

    def finish(n, base, with_centre):
        w_copy(0, n).wait()
        w_copy(2, n).wait()
        if with_centre:
            w_copy(1, n).wait()
        cols = pl.ds(pl.multiple_of(n * CHUNK, CHUNK), CHUNK)
        total = dot(xbuf[0:rows], wbuf[n, 0]) + dot(xbuf[2 * halo : 2 * halo + rows], wbuf[n, 2])
        if with_centre:
            total = total + dot(xbuf[halo : halo + rows], wbuf[n, 1])
        else:
            total = total + base
        half = 0.5 * total
        hidden = (xbuf[halo : halo + rows, cols].astype(F32) + (half + half * jnp.tanh(half))).astype(BF16)
        pooled[:, cols] = jnp.sum(hidden.astype(F32).reshape(bins, POOL, CHUNK), axis=1) * (1.0 / POOL)
        emb_acc[...] += dot(hidden, donor_ref[cols, :])

    def first(n, carry):
        finish(n, early[n], False)
        return carry

    def rest(n, carry):
        finish(n, None, True)
        return carry

    lax.fori_loop(0, pre, first, 0)
    lax.fori_loop(pre, chunks, rest, 0)

    means = pooled[...]
    scale = lax.rsqrt(jnp.mean(means * means, axis=-1, keepdims=True) + 1e-06)
    projected = dot((means * scale).astype(BF16), proj_ref[...]).astype(BF16).astype(F32)
    row_send[...] = projected[:, :LANES]
    col_send[...] = projected[:, LANES:]

    my_slot = me - col_home * n_row

    def col_copy(r):
        return pltpu.make_async_remote_copy(
            src_ref=col_send,
            dst_ref=cols_out.at[my_slot],
            send_sem=col_send_sem.at[r],
            recv_sem=col_recv_sem.at[my_slot],
            device_id=(r, col_home),
            device_id_type=MESH,
        )

    def is_other(r):
        return jnp.logical_or(jnp.logical_not(self_col), my_row != r)

    for r in range(n_row):

        @pl.when(is_other(r))
        def _():
            col_copy(r).start()

    row_copies = row_group_copies(row_send, rows_out, row_send_sem, row_recv_sem, True)
    for copy in row_copies:
        copy.start()

    emb_send[...] = dot(select[...], emb_acc[...].astype(BF16)).astype(BF16).reshape(n_col, CAP, LANES)
    emb_copies = row_group_copies(emb_send, emb_out, emb_send_sem, emb_recv_sem, False)
    for copy in emb_copies:
        copy.start()
    emb_out[my_col] = emb_send[my_col]
    rows_out[my_col] = row_send[...]

    @pl.when(self_col)
    def _():
        cols_out[my_slot] = col_send[...]

    row_group_arrivals(coord_send.at[0], coord_out, coord_send_sem, coord_recv_sem)
    row_group_arrivals(row_send, rows_out, row_send_sem, row_recv_sem)
    row_group_arrivals(emb_send.at[0], emb_out, emb_send_sem, emb_recv_sem)
    for i in range(n_row):
        source = my_col * n_row + i

        @pl.when(source != me)
        def _():
            pltpu.make_async_remote_copy(
                src_ref=col_send,
                dst_ref=cols_out.at[i],
                send_sem=col_send_sem.at[i],
                recv_sem=col_recv_sem.at[i],
                device_id=place(source),
                device_id_type=MESH,
            ).wait_recv()

    for copy in coord_copies + row_copies + emb_copies:
        copy.wait_send()
    for r in range(n_row):

        @pl.when(is_other(r))
        def _():
            col_copy(r).wait_send()

    @pl.when(has_left)
    def _():
        up_copy().wait_send()

    @pl.when(has_right)
    def _():
        down_copy().wait_send()


def tiles(rows_ref, cols_ref, emb_ref, coord_ref, out_ref, pair_ref, junction_ref):
    n_col, bins, lanes = rows_ref.shape
    n_row = cols_ref.shape[0]
    tile_rows, tile_cols = n_col * bins, n_row * bins
    row_side = rows_ref[...].reshape(tile_rows, lanes)
    col_side = cols_ref[...].reshape(tile_cols, lanes)
    weight = out_ref[...]
    cap = emb_ref.shape[1]
    col_lanes = coord_ref.shape[2] - lanes
    side = min(8, tile_rows)
    for i in range(tile_rows // side):
        hidden = jnp.maximum(row_side[i * side : (i + 1) * side, None, :] + col_side[None, :, :], 0.0).astype(BF16)
        pair_ref[i * side : (i + 1) * side] = (
            dot(hidden.reshape(side * tile_cols, lanes), weight).astype(BF16).reshape(side, tile_cols, lanes)
        )
    coord = coord_ref[...]
    by_col = dot(coord[:, :, :tile_cols].reshape(n_col * cap, tile_cols), col_side.astype(BF16))
    by_row = [dot(coord[k, :, col_lanes : col_lanes + bins], rows_ref[k].astype(BF16)) for k in range(n_col)]
    hidden = jnp.maximum(jnp.concatenate(by_row, axis=0) + by_col, 0.0).astype(BF16)
    looked = dot(hidden, weight).astype(BF16)
    emb = emb_ref[...].reshape(n_col * cap, lanes)
    junction_ref[...] = jnp.maximum(emb.astype(F32) + looked.astype(F32), 0.0).astype(BF16)


def local(n_row, n_col, sequence, filter_weight, pair_proj, pair_out, donor_w, donor_pos, acceptor_bin):
    rows, width = sequence.shape
    lanes = pair_out.shape[0]
    bins = rows // POOL
    listed = donor_pos.shape[0]
    chunks = width // CHUNK
    tile_rows, tile_cols = bins * n_col, bins * n_row
    col_lanes = -(-tile_cols // LANES) * LANES
    slots = n_col * CAP
    vmem = pl.BlockSpec(memory_space=pltpu.VMEM)
    hbm = pl.BlockSpec(memory_space=pl.ANY)
    dma = pltpu.SemaphoreType.DMA
    arrived = pl.pallas_call(
        functools.partial(trunk, n_row, n_col),
        out_shape=(
            jax.ShapeDtypeStruct((n_col, bins, lanes), F32),
            jax.ShapeDtypeStruct((n_row, bins, lanes), F32),
            jax.ShapeDtypeStruct((n_col, CAP, lanes), BF16),
            jax.ShapeDtypeStruct((n_col, CAP, col_lanes + LANES), BF16),
        ),
        in_specs=[hbm, hbm, vmem, vmem, vmem, vmem],
        out_specs=(vmem, vmem, vmem, vmem),
        scratch_shapes=[
            pltpu.VMEM((rows + 2 * DILATION_STEP, width), BF16),
            pltpu.VMEM((chunks, 3, width, CHUNK), BF16),
            pltpu.VMEM((min(PRE, chunks), rows, CHUNK), F32),
            pltpu.VMEM((rows, lanes), F32),
            pltpu.VMEM((bins, width), F32),
            pltpu.VMEM((slots, rows), BF16),
            pltpu.VMEM((bins, lanes), F32),
            pltpu.VMEM((bins, lanes), F32),
            pltpu.VMEM((n_col, CAP, lanes), BF16),
            pltpu.VMEM((n_col, CAP, col_lanes + LANES), BF16),
            dma,
            dma((chunks, 3)),
            dma((2,)),
            dma((2,)),
            dma((n_col - 1,)),
            dma((n_col - 1,)),
            dma((n_col - 1,)),
            dma((n_col - 1,)),
            dma((n_col - 1,)),
            dma((n_col - 1,)),
            dma((n_row,)),
            dma((n_row,)),
        ],
        compiler_params=pltpu.CompilerParams(
            collective_id=0, has_side_effects=True, vmem_limit_bytes=56 * 1024 * 1024
        ),
        name="trunk",
    )(
        sequence,
        filter_weight,
        pair_proj,
        donor_w,
        donor_pos.reshape(1, listed),
        acceptor_bin.reshape(1, listed),
    )
    return pl.pallas_call(
        tiles,
        out_shape=(
            jax.ShapeDtypeStruct((tile_rows, tile_cols, lanes), BF16),
            jax.ShapeDtypeStruct((slots, lanes), BF16),
        ),
        in_specs=[vmem] * 5,
        out_specs=(vmem, vmem),
        name="tiles",
    )(*arrived, pair_out)


def solution(mesh):
    placed = (P(("row", "col"), None), P(), P(), P(), P(), P(("row", "col")), P(("row", "col")))
    return jax.shard_map(
        functools.partial(local, mesh.shape["row"], mesh.shape["col"]),
        mesh=mesh,
        in_specs=placed,
        out_specs=(P("row", "col", None), P(("row", "col"), None)),
        check_vma=False,
    )
```

```python
import functools

import jax
import jax.numpy as jnp
from jax import lax
from jax.experimental import pallas as pl
from jax.experimental.pallas import tpu as pltpu
from jax.sharding import PartitionSpec as P

DILATION_STEP = 32
POOL = 128
CAP = 64
LANES = 128
CHUNK = 512
BLOCK = 256
PRE = 1
MESH = pl.DeviceIdType.MESH
F32 = jnp.float32
BF16 = jnp.bfloat16


def dot(a, b):
    return jnp.dot(a, b, preferred_element_type=F32)


def trunk(
    n_row,
    n_col,
    x_hbm,
    w_hbm,
    proj_hbm,
    donor_hbm,
    pos_ref,
    bin_ref,
    rows_out,
    cols_out,
    emb_out,
    coord_out,
    xbuf,
    wbuf,
    hidden,
    pooled,
    select,
    proj_ref,
    donor_ref,
    row_send,
    col_send,
    emb_send,
    coord_send,
    x_sem,
    end_sem,
    w_sem,
    halo_send_sem,
    halo_recv_sem,
    coord_send_sem,
    coord_recv_sem,
    emb_send_sem,
    emb_recv_sem,
    row_send_sem,
    row_recv_sem,
    col_send_sem,
    col_recv_sem,
):
    rows, width = x_hbm.shape
    halo = DILATION_STEP
    chunks = width // CHUNK
    pre = min(PRE, chunks)
    bins = rows // POOL
    tile_cols = bins * n_row
    slots = n_col * CAP
    count = n_row * n_col
    my_row = lax.axis_index("row")
    my_col = lax.axis_index("col")
    me = my_row * n_col + my_col

    def place(flat):
        return (flat // n_col, lax.rem(flat, n_col))

    def w_copy(tap, n):
        return pltpu.make_async_copy(
            w_hbm.at[tap, :, pl.ds(pl.multiple_of(n * CHUNK, CHUNK), CHUNK)], wbuf.at[n, pl.ds(tap * width, width)], w_sem.at[n, tap]
        )

    x_copy = pltpu.make_async_copy(x_hbm, xbuf.at[pl.ds(halo, rows)], x_sem)
    x_copy.start()
    for n in range(chunks):
        for tap in range(3):
            w_copy(tap, n).start()
    proj_copy = pltpu.make_async_copy(proj_hbm, proj_ref, end_sem.at[0])
    donor_copy = pltpu.make_async_copy(donor_hbm, donor_ref, end_sem.at[1])
    proj_copy.start()
    donor_copy.start()

    has_left = me > 0
    has_right = me < count - 1
    col_home = me // n_row
    self_col = col_home == my_col
    barrier = pltpu.get_barrier_semaphore()

    @pl.when(has_left)
    def _():
        pl.semaphore_signal(barrier, inc=1, device_id=place(me - 1), device_id_type=MESH)

    @pl.when(has_right)
    def _():
        pl.semaphore_signal(barrier, inc=1, device_id=place(me + 1), device_id_type=MESH)

    for d in range(1, n_col):
        pl.semaphore_signal(barrier, inc=1, device_id=(my_row, lax.rem(my_col + d, n_col)), device_id_type=MESH)
    for i in range(n_row):
        source = my_col * n_row + i

        @pl.when(source != me)
        def _():
            pl.semaphore_signal(barrier, inc=1, device_id=place(source), device_id_type=MESH)

    pos = pos_ref[...]
    acceptor = bin_ref[...]
    listed = pos.shape[1]
    group = jnp.zeros_like(acceptor)
    for k in range(1, n_col):
        group = group + jnp.where(acceptor >= k * tile_cols, 1, 0)
    pair_col = acceptor - group * tile_cols
    kinds = max(16, n_col)
    in_group = lax.broadcasted_iota(jnp.int32, (kinds, listed), 0) == group
    before = lax.broadcasted_iota(jnp.int32, (listed, listed), 0) < lax.broadcasted_iota(jnp.int32, (listed, listed), 1)
    in_group = jnp.where(in_group, 1.0, 0.0)
    earlier = dot(in_group.astype(BF16), jnp.where(before, 1.0, 0.0).astype(BF16))
    rank = jnp.sum(in_group * earlier, axis=0, keepdims=True)
    slot = group.astype(F32) * float(CAP) + rank
    slot_hot = lax.broadcasted_iota(jnp.int32, (slots, listed), 0).astype(F32) == slot
    slot_hot = jnp.where(slot_hot, 1.0, 0.0).astype(BF16)

    def spread(hot):
        return lax.dot_general(
            slot_hot, jnp.where(hot, 1.0, 0.0).astype(BF16), (((1,), (1,)), ((), ())), preferred_element_type=F32
        ).astype(BF16)

    col_lanes = coord_send.shape[2] - LANES
    col_hot = lax.broadcasted_iota(jnp.int32, (col_lanes, listed), 0) == pair_col
    coord_send[:, :, :col_lanes] = spread(col_hot).reshape(n_col, CAP, col_lanes)
    base = lax.broadcasted_iota(jnp.int32, (LANES, listed), 0) * POOL
    row_hot = (pos >= base) & (pos < base + POOL)
    coord_send[:, :, col_lanes:] = spread(row_hot).reshape(n_col, CAP, LANES)
    select[...] = spread(lax.broadcasted_iota(jnp.int32, (rows, listed), 0) == pos)

    neighbours = jnp.where(has_left, 1, 0) + jnp.where(has_right, 1, 0)
    pl.semaphore_wait(barrier, neighbours + n_col - 1 + n_row - jnp.where(self_col, 1, 0))

    def up_copy():
        return pltpu.make_async_remote_copy(
            src_ref=x_hbm.at[pl.ds(0, halo)],
            dst_ref=xbuf.at[pl.ds(rows + halo, halo)],
            send_sem=halo_send_sem.at[0],
            recv_sem=halo_recv_sem.at[0],
            device_id=place(me - 1),
            device_id_type=MESH,
        )

    def down_copy():
        return pltpu.make_async_remote_copy(
            src_ref=x_hbm.at[pl.ds(rows - halo, halo)],
            dst_ref=xbuf.at[pl.ds(0, halo)],
            send_sem=halo_send_sem.at[1],
            recv_sem=halo_recv_sem.at[1],
            device_id=place(me + 1),
            device_id_type=MESH,
        )

    def row_group_copies(src, dst, send_sem, recv_sem, whole):
        copies = []
        for d in range(1, n_col):
            there = lax.rem(my_col + d, n_col)
            copies.append(
                pltpu.make_async_remote_copy(
                    src_ref=src if whole else src.at[there],
                    dst_ref=dst.at[my_col],
                    send_sem=send_sem.at[d - 1],
                    recv_sem=recv_sem.at[d - 1],
                    device_id=(my_row, there),
                    device_id_type=MESH,
                )
            )
        return copies

    def row_group_arrivals(src, dst, send_sem, recv_sem):
        for d in range(1, n_col):
            source = lax.rem(my_col + n_col - d, n_col)
            pltpu.make_async_remote_copy(
                src_ref=src,
                dst_ref=dst.at[source],
                send_sem=send_sem.at[d - 1],
                recv_sem=recv_sem.at[d - 1],
                device_id=(my_row, source),
                device_id_type=MESH,
            ).wait_recv()

    @pl.when(has_left)
    def _():
        up_copy().start()

    @pl.when(has_right)
    def _():
        down_copy().start()

    coord_copies = row_group_copies(coord_send, coord_out, coord_send_sem, coord_recv_sem, False)
    for copy in coord_copies:
        copy.start()
    coord_out[my_col] = coord_send[my_col]

    @pl.when(jnp.logical_not(has_left))
    def _():
        xbuf[0:halo] = jnp.zeros((halo, width), BF16)

    @pl.when(jnp.logical_not(has_right))
    def _():
        xbuf[rows + halo : rows + 2 * halo] = jnp.zeros((halo, width), BF16)

    x_copy.wait()

    def block(n, start):
        cols = pl.ds(pl.multiple_of(n * CHUNK, CHUNK), CHUNK)
        taps = [xbuf[start + tap * halo : start + tap * halo + BLOCK] for tap in range(3)]
        total = dot(jnp.concatenate(taps, axis=1), wbuf[n])
        half = 0.5 * total
        centre = xbuf[start + halo : start + halo + BLOCK, cols].astype(F32)
        out = (centre + (half + half * jnp.tanh(half))).astype(BF16)
        hidden[start : start + BLOCK, cols] = out
        first = start // POOL
        pooled[first : first + BLOCK // POOL, cols] = jnp.sum(
            out.astype(F32).reshape(BLOCK // POOL, POOL, CHUNK), axis=1
        ) * (1.0 / POOL)

    starts = list(range(0, rows, BLOCK))

    def inner(n, carry):
        for tap in range(3):
            w_copy(tap, n).wait()
        for start in starts[1:-1]:
            block(n, start)
        return carry

    lax.fori_loop(0, pre, inner, 0)

    @pl.when(has_left)
    def _():
        down_copy().wait_recv()

    @pl.when(has_right)
    def _():
        up_copy().wait_recv()

    def outer(n, carry):
        for start in (starts[0], starts[-1]):
            block(n, start)
        return carry

    def rest(n, carry):
        for tap in range(3):
            w_copy(tap, n).wait()
        for start in starts:
            block(n, start)
        return carry

    lax.fori_loop(0, pre, outer, 0)
    lax.fori_loop(pre, chunks, rest, 0)

    proj_copy.wait()
    donor_copy.wait()
    means = pooled[...]
    scale = lax.rsqrt(jnp.mean(means * means, axis=-1, keepdims=True) + 1e-06)
    projected = dot((means * scale).astype(BF16), proj_ref[...]).astype(BF16).astype(F32)
    row_send[...] = projected[:, :LANES]
    col_send[...] = projected[:, LANES:]

    my_slot = me - col_home * n_row

    def col_copy(r):
        return pltpu.make_async_remote_copy(
            src_ref=col_send,
            dst_ref=cols_out.at[my_slot],
            send_sem=col_send_sem.at[r],
            recv_sem=col_recv_sem.at[my_slot],
            device_id=(r, col_home),
            device_id_type=MESH,
        )

    def is_other(r):
        return jnp.logical_or(jnp.logical_not(self_col), my_row != r)

    for r in range(n_row):

        @pl.when(is_other(r))
        def _():
            col_copy(r).start()

    row_copies = row_group_copies(row_send, rows_out, row_send_sem, row_recv_sem, True)
    for copy in row_copies:
        copy.start()

    emb_send[...] = dot(select[...], dot(hidden[...], donor_ref[...]).astype(BF16)).astype(BF16).reshape(n_col, CAP, LANES)
    emb_copies = row_group_copies(emb_send, emb_out, emb_send_sem, emb_recv_sem, False)
    for copy in emb_copies:
        copy.start()
    emb_out[my_col] = emb_send[my_col]
    rows_out[my_col] = row_send[...]

    @pl.when(self_col)
    def _():
        cols_out[my_slot] = col_send[...]

    row_group_arrivals(coord_send.at[0], coord_out, coord_send_sem, coord_recv_sem)
    row_group_arrivals(row_send, rows_out, row_send_sem, row_recv_sem)
    row_group_arrivals(emb_send.at[0], emb_out, emb_send_sem, emb_recv_sem)
    for i in range(n_row):
        source = my_col * n_row + i

        @pl.when(source != me)
        def _():
            pltpu.make_async_remote_copy(
                src_ref=col_send,
                dst_ref=cols_out.at[i],
                send_sem=col_send_sem.at[i],
                recv_sem=col_recv_sem.at[i],
                device_id=place(source),
                device_id_type=MESH,
            ).wait_recv()

    for copy in coord_copies + row_copies + emb_copies:
        copy.wait_send()
    for r in range(n_row):

        @pl.when(is_other(r))
        def _():
            col_copy(r).wait_send()

    @pl.when(has_left)
    def _():
        up_copy().wait_send()

    @pl.when(has_right)
    def _():
        down_copy().wait_send()


def tiles(rows_ref, cols_ref, emb_ref, coord_ref, out_ref, pair_ref, junction_ref):
    n_col, bins, lanes = rows_ref.shape
    n_row = cols_ref.shape[0]
    tile_rows, tile_cols = n_col * bins, n_row * bins
    row_side = rows_ref[...].reshape(tile_rows, lanes)
    col_side = cols_ref[...].reshape(tile_cols, lanes)
    weight = out_ref[...]
    cap = emb_ref.shape[1]
    col_lanes = coord_ref.shape[2] - lanes
    side = min(8, tile_rows)
    for i in range(tile_rows // side):
        hidden = jnp.maximum(row_side[i * side : (i + 1) * side, None, :] + col_side[None, :, :], 0.0).astype(BF16)
        pair_ref[i * side : (i + 1) * side] = (
            dot(hidden.reshape(side * tile_cols, lanes), weight).astype(BF16).reshape(side, tile_cols, lanes)
        )
    coord = coord_ref[...]
    by_col = dot(coord[:, :, :tile_cols].reshape(n_col * cap, tile_cols), col_side.astype(BF16))
    by_row = [dot(coord[k, :, col_lanes : col_lanes + bins], rows_ref[k].astype(BF16)) for k in range(n_col)]
    hidden = jnp.maximum(jnp.concatenate(by_row, axis=0) + by_col, 0.0).astype(BF16)
    looked = dot(hidden, weight).astype(BF16)
    emb = emb_ref[...].reshape(n_col * cap, lanes)
    junction_ref[...] = jnp.maximum(emb.astype(F32) + looked.astype(F32), 0.0).astype(BF16)


def local(n_row, n_col, sequence, filter_weight, pair_proj, pair_out, donor_w, donor_pos, acceptor_bin):
    rows, width = sequence.shape
    lanes = pair_out.shape[0]
    bins = rows // POOL
    listed = donor_pos.shape[0]
    chunks = width // CHUNK
    tile_rows, tile_cols = bins * n_col, bins * n_row
    col_lanes = -(-tile_cols // LANES) * LANES
    slots = n_col * CAP
    vmem = pl.BlockSpec(memory_space=pltpu.VMEM)
    hbm = pl.BlockSpec(memory_space=pl.ANY)
    dma = pltpu.SemaphoreType.DMA
    arrived = pl.pallas_call(
        functools.partial(trunk, n_row, n_col),
        out_shape=(
            jax.ShapeDtypeStruct((n_col, bins, lanes), F32),
            jax.ShapeDtypeStruct((n_row, bins, lanes), F32),
            jax.ShapeDtypeStruct((n_col, CAP, lanes), BF16),
            jax.ShapeDtypeStruct((n_col, CAP, col_lanes + LANES), BF16),
        ),
        in_specs=[hbm, hbm, hbm, hbm, vmem, vmem],
        out_specs=(vmem, vmem, vmem, vmem),
        scratch_shapes=[
            pltpu.VMEM((rows + 2 * DILATION_STEP, width), BF16),
            pltpu.VMEM((chunks, 3 * width, CHUNK), BF16),
            pltpu.VMEM((rows, width), BF16),
            pltpu.VMEM((bins, width), F32),
            pltpu.VMEM((slots, rows), BF16),
            pltpu.VMEM(pair_proj.shape, BF16),
            pltpu.VMEM(donor_w.shape, BF16),
            pltpu.VMEM((bins, lanes), F32),
            pltpu.VMEM((bins, lanes), F32),
            pltpu.VMEM((n_col, CAP, lanes), BF16),
            pltpu.VMEM((n_col, CAP, col_lanes + LANES), BF16),
            dma,
            dma((2,)),
            dma((chunks, 3)),
            dma((2,)),
            dma((2,)),
            dma((n_col - 1,)),
            dma((n_col - 1,)),
            dma((n_col - 1,)),
            dma((n_col - 1,)),
            dma((n_col - 1,)),
            dma((n_col - 1,)),
            dma((n_row,)),
            dma((n_row,)),
        ],
        compiler_params=pltpu.CompilerParams(
            collective_id=0, has_side_effects=True, vmem_limit_bytes=56 * 1024 * 1024
        ),
        name="trunk",
    )(
        sequence,
        filter_weight,
        pair_proj,
        donor_w,
        donor_pos.reshape(1, listed),
        acceptor_bin.reshape(1, listed),
    )
    return pl.pallas_call(
        tiles,
        out_shape=(
            jax.ShapeDtypeStruct((tile_rows, tile_cols, lanes), BF16),
            jax.ShapeDtypeStruct((slots, lanes), BF16),
        ),
        in_specs=[vmem] * 5,
        out_specs=(vmem, vmem),
        name="tiles",
    )(*arrived, pair_out)


def solution(mesh):
    placed = (P(("row", "col"), None), P(), P(), P(), P(), P(("row", "col")), P(("row", "col")))
    return jax.shard_map(
        functools.partial(local, mesh.shape["row"], mesh.shape["col"]),
        mesh=mesh,
        in_specs=placed,
        out_specs=(P("row", "col", None), P(("row", "col"), None)),
        check_vma=False,
    )
```

```python
import functools

import jax
import jax.numpy as jnp
from jax import lax
from jax.experimental import pallas as pl
from jax.experimental.pallas import tpu as pltpu
from jax.sharding import PartitionSpec as P

DILATION_STEP = 32
POOL = 128
CAP = 64
LANES = 128
CHUNK = 512
BLOCK = 256
PRE = 2
MESH = pl.DeviceIdType.MESH
F32 = jnp.float32
BF16 = jnp.bfloat16


def dot(a, b):
    return jnp.dot(a, b, preferred_element_type=F32)


def trunk(
    n_row,
    n_col,
    x_hbm,
    w_hbm,
    proj_hbm,
    donor_hbm,
    pos_ref,
    bin_ref,
    rows_out,
    cols_out,
    emb_out,
    coord_out,
    xbuf,
    wbuf,
    hidden,
    pooled,
    select,
    proj_ref,
    donor_ref,
    row_send,
    col_send,
    emb_send,
    coord_send,
    x_sem,
    end_sem,
    w_sem,
    halo_send_sem,
    halo_recv_sem,
    coord_send_sem,
    coord_recv_sem,
    emb_send_sem,
    emb_recv_sem,
    row_send_sem,
    row_recv_sem,
    col_send_sem,
    col_recv_sem,
):
    rows, width = x_hbm.shape
    halo = DILATION_STEP
    chunks = width // CHUNK
    pre = min(PRE, chunks)
    bins = rows // POOL
    tile_cols = bins * n_row
    slots = n_col * CAP
    count = n_row * n_col
    my_row = lax.axis_index("row")
    my_col = lax.axis_index("col")
    me = my_row * n_col + my_col

    def place(flat):
        return (flat // n_col, lax.rem(flat, n_col))

    has_left = me > 0
    has_right = me < count - 1
    col_home = me // n_row
    self_col = col_home == my_col
    barrier = pltpu.get_barrier_semaphore()

    @pl.when(has_left)
    def _():
        pl.semaphore_signal(barrier, inc=1, device_id=place(me - 1), device_id_type=MESH)

    @pl.when(has_right)
    def _():
        pl.semaphore_signal(barrier, inc=1, device_id=place(me + 1), device_id_type=MESH)

    for d in range(1, n_col):
        pl.semaphore_signal(barrier, inc=1, device_id=(my_row, lax.rem(my_col + d, n_col)), device_id_type=MESH)
    for i in range(n_row):
        source = my_col * n_row + i

        @pl.when(source != me)
        def _():
            pl.semaphore_signal(barrier, inc=1, device_id=place(source), device_id_type=MESH)

    def w_copy(tap, n):
        return pltpu.make_async_copy(
            w_hbm.at[tap, :, pl.ds(pl.multiple_of(n * CHUNK, CHUNK), CHUNK)], wbuf.at[n, pl.ds(tap * width, width)], w_sem.at[n, tap]
        )

    x_copy = pltpu.make_async_copy(x_hbm, xbuf.at[pl.ds(halo, rows)], x_sem)
    x_copy.start()
    for n in range(chunks):
        for tap in range(3):
            w_copy(tap, n).start()
    proj_copy = pltpu.make_async_copy(proj_hbm, proj_ref, end_sem.at[0])
    donor_copy = pltpu.make_async_copy(donor_hbm, donor_ref, end_sem.at[1])
    proj_copy.start()
    donor_copy.start()

    pos = pos_ref[...]
    acceptor = bin_ref[...]
    listed = pos.shape[1]
    group = jnp.zeros_like(acceptor)
    for k in range(1, n_col):
        group = group + jnp.where(acceptor >= k * tile_cols, 1, 0)
    pair_col = acceptor - group * tile_cols
    kinds = max(16, n_col)
    in_group = lax.broadcasted_iota(jnp.int32, (kinds, listed), 0) == group
    before = lax.broadcasted_iota(jnp.int32, (listed, listed), 0) < lax.broadcasted_iota(jnp.int32, (listed, listed), 1)
    in_group = jnp.where(in_group, 1.0, 0.0)
    earlier = dot(in_group.astype(BF16), jnp.where(before, 1.0, 0.0).astype(BF16))
    rank = jnp.sum(in_group * earlier, axis=0, keepdims=True)
    slot = group.astype(F32) * float(CAP) + rank
    slot_hot = lax.broadcasted_iota(jnp.int32, (slots, listed), 0).astype(F32) == slot
    slot_hot = jnp.where(slot_hot, 1.0, 0.0).astype(BF16)

    def spread(hot):
        return lax.dot_general(
            slot_hot, jnp.where(hot, 1.0, 0.0).astype(BF16), (((1,), (1,)), ((), ())), preferred_element_type=F32
        ).astype(BF16)

    col_lanes = coord_send.shape[2] - LANES
    col_hot = lax.broadcasted_iota(jnp.int32, (col_lanes, listed), 0) == pair_col
    coord_send[:, :, :col_lanes] = spread(col_hot).reshape(n_col, CAP, col_lanes)
    base = lax.broadcasted_iota(jnp.int32, (LANES, listed), 0) * POOL
    row_hot = (pos >= base) & (pos < base + POOL)
    coord_send[:, :, col_lanes:] = spread(row_hot).reshape(n_col, CAP, LANES)
    select[...] = spread(lax.broadcasted_iota(jnp.int32, (rows, listed), 0) == pos)

    neighbours = jnp.where(has_left, 1, 0) + jnp.where(has_right, 1, 0)
    pl.semaphore_wait(barrier, neighbours + n_col - 1 + n_row - jnp.where(self_col, 1, 0))

    def up_copy():
        return pltpu.make_async_remote_copy(
            src_ref=x_hbm.at[pl.ds(0, halo)],
            dst_ref=xbuf.at[pl.ds(rows + halo, halo)],
            send_sem=halo_send_sem.at[0],
            recv_sem=halo_recv_sem.at[0],
            device_id=place(me - 1),
            device_id_type=MESH,
        )

    def down_copy():
        return pltpu.make_async_remote_copy(
            src_ref=x_hbm.at[pl.ds(rows - halo, halo)],
            dst_ref=xbuf.at[pl.ds(0, halo)],
            send_sem=halo_send_sem.at[1],
            recv_sem=halo_recv_sem.at[1],
            device_id=place(me + 1),
            device_id_type=MESH,
        )

    def row_group_copies(src, dst, send_sem, recv_sem, whole):
        copies = []
        for d in range(1, n_col):
            there = lax.rem(my_col + d, n_col)
            copies.append(
                pltpu.make_async_remote_copy(
                    src_ref=src if whole else src.at[there],
                    dst_ref=dst.at[my_col],
                    send_sem=send_sem.at[d - 1],
                    recv_sem=recv_sem.at[d - 1],
                    device_id=(my_row, there),
                    device_id_type=MESH,
                )
            )
        return copies

    def row_group_arrivals(src, dst, send_sem, recv_sem):
        for d in range(1, n_col):
            source = lax.rem(my_col + n_col - d, n_col)
            pltpu.make_async_remote_copy(
                src_ref=src,
                dst_ref=dst.at[source],
                send_sem=send_sem.at[d - 1],
                recv_sem=recv_sem.at[d - 1],
                device_id=(my_row, source),
                device_id_type=MESH,
            ).wait_recv()

    @pl.when(has_left)
    def _():
        up_copy().start()

    @pl.when(has_right)
    def _():
        down_copy().start()

    coord_copies = row_group_copies(coord_send, coord_out, coord_send_sem, coord_recv_sem, False)
    for copy in coord_copies:
        copy.start()
    coord_out[my_col] = coord_send[my_col]

    @pl.when(jnp.logical_not(has_left))
    def _():
        xbuf[0:halo] = jnp.zeros((halo, width), BF16)

    @pl.when(jnp.logical_not(has_right))
    def _():
        xbuf[rows + halo : rows + 2 * halo] = jnp.zeros((halo, width), BF16)

    x_copy.wait()

    def block(n, start):
        cols = pl.ds(pl.multiple_of(n * CHUNK, CHUNK), CHUNK)
        taps = [xbuf[start + tap * halo : start + tap * halo + BLOCK] for tap in range(3)]
        total = dot(jnp.concatenate(taps, axis=1), wbuf[n])
        half = 0.5 * total
        centre = xbuf[start + halo : start + halo + BLOCK, cols].astype(F32)
        out = (centre + (half + half * jnp.tanh(half))).astype(BF16)
        hidden[start : start + BLOCK, cols] = out
        first = start // POOL
        pooled[first : first + BLOCK // POOL, cols] = jnp.sum(
            out.astype(F32).reshape(BLOCK // POOL, POOL, CHUNK), axis=1
        ) * (1.0 / POOL)

    starts = list(range(0, rows, BLOCK))

    def inner(n, carry):
        for tap in range(3):
            w_copy(tap, n).wait()
        for start in starts[1:-1]:
            block(n, start)
        return carry

    lax.fori_loop(0, pre, inner, 0)

    @pl.when(has_left)
    def _():
        down_copy().wait_recv()

    @pl.when(has_right)
    def _():
        up_copy().wait_recv()

    def outer(n, carry):
        for start in (starts[0], starts[-1]):
            block(n, start)
        return carry

    def rest(n, carry):
        for tap in range(3):
            w_copy(tap, n).wait()
        for start in starts:
            block(n, start)
        return carry

    lax.fori_loop(0, pre, outer, 0)
    lax.fori_loop(pre, chunks, rest, 0)

    proj_copy.wait()
    donor_copy.wait()
    means = pooled[...]
    scale = lax.rsqrt(jnp.mean(means * means, axis=-1, keepdims=True) + 1e-06)
    projected = dot((means * scale).astype(BF16), proj_ref[...]).astype(BF16).astype(F32)
    row_send[...] = projected[:, :LANES]
    col_send[...] = projected[:, LANES:]

    my_slot = me - col_home * n_row

    def col_copy(r):
        return pltpu.make_async_remote_copy(
            src_ref=col_send,
            dst_ref=cols_out.at[my_slot],
            send_sem=col_send_sem.at[r],
            recv_sem=col_recv_sem.at[my_slot],
            device_id=(r, col_home),
            device_id_type=MESH,
        )

    def is_other(r):
        return jnp.logical_or(jnp.logical_not(self_col), my_row != r)

    for r in range(n_row):

        @pl.when(is_other(r))
        def _():
            col_copy(r).start()

    row_copies = row_group_copies(row_send, rows_out, row_send_sem, row_recv_sem, True)
    for copy in row_copies:
        copy.start()

    emb_send[...] = dot(select[...], dot(hidden[...], donor_ref[...]).astype(BF16)).astype(BF16).reshape(n_col, CAP, LANES)
    emb_copies = row_group_copies(emb_send, emb_out, emb_send_sem, emb_recv_sem, False)
    for copy in emb_copies:
        copy.start()
    emb_out[my_col] = emb_send[my_col]
    rows_out[my_col] = row_send[...]

    @pl.when(self_col)
    def _():
        cols_out[my_slot] = col_send[...]

    row_group_arrivals(coord_send.at[0], coord_out, coord_send_sem, coord_recv_sem)
    row_group_arrivals(row_send, rows_out, row_send_sem, row_recv_sem)
    row_group_arrivals(emb_send.at[0], emb_out, emb_send_sem, emb_recv_sem)
    for i in range(n_row):
        source = my_col * n_row + i

        @pl.when(source != me)
        def _():
            pltpu.make_async_remote_copy(
                src_ref=col_send,
                dst_ref=cols_out.at[i],
                send_sem=col_send_sem.at[i],
                recv_sem=col_recv_sem.at[i],
                device_id=place(source),
                device_id_type=MESH,
            ).wait_recv()

    for copy in coord_copies + row_copies + emb_copies:
        copy.wait_send()
    for r in range(n_row):

        @pl.when(is_other(r))
        def _():
            col_copy(r).wait_send()

    @pl.when(has_left)
    def _():
        up_copy().wait_send()

    @pl.when(has_right)
    def _():
        down_copy().wait_send()


def tiles(rows_ref, cols_ref, emb_ref, coord_ref, out_ref, pair_ref, junction_ref):
    n_col, bins, lanes = rows_ref.shape
    n_row = cols_ref.shape[0]
    tile_rows, tile_cols = n_col * bins, n_row * bins
    row_side = rows_ref[...].reshape(tile_rows, lanes)
    col_side = cols_ref[...].reshape(tile_cols, lanes)
    weight = out_ref[...]
    cap = emb_ref.shape[1]
    col_lanes = coord_ref.shape[2] - lanes
    side = min(8, tile_rows)
    for i in range(tile_rows // side):
        hidden = jnp.maximum(row_side[i * side : (i + 1) * side, None, :] + col_side[None, :, :], 0.0).astype(BF16)
        pair_ref[i * side : (i + 1) * side] = (
            dot(hidden.reshape(side * tile_cols, lanes), weight).astype(BF16).reshape(side, tile_cols, lanes)
        )
    coord = coord_ref[...]
    by_col = dot(coord[:, :, :tile_cols].reshape(n_col * cap, tile_cols), col_side.astype(BF16))
    by_row = [dot(coord[k, :, col_lanes : col_lanes + bins], rows_ref[k].astype(BF16)) for k in range(n_col)]
    hidden = jnp.maximum(jnp.concatenate(by_row, axis=0) + by_col, 0.0).astype(BF16)
    looked = dot(hidden, weight).astype(BF16)
    emb = emb_ref[...].reshape(n_col * cap, lanes)
    junction_ref[...] = jnp.maximum(emb.astype(F32) + looked.astype(F32), 0.0).astype(BF16)


def local(n_row, n_col, sequence, filter_weight, pair_proj, pair_out, donor_w, donor_pos, acceptor_bin):
    rows, width = sequence.shape
    lanes = pair_out.shape[0]
    bins = rows // POOL
    listed = donor_pos.shape[0]
    chunks = width // CHUNK
    tile_rows, tile_cols = bins * n_col, bins * n_row
    col_lanes = -(-tile_cols // LANES) * LANES
    slots = n_col * CAP
    vmem = pl.BlockSpec(memory_space=pltpu.VMEM)
    hbm = pl.BlockSpec(memory_space=pl.ANY)
    dma = pltpu.SemaphoreType.DMA
    arrived = pl.pallas_call(
        functools.partial(trunk, n_row, n_col),
        out_shape=(
            jax.ShapeDtypeStruct((n_col, bins, lanes), F32),
            jax.ShapeDtypeStruct((n_row, bins, lanes), F32),
            jax.ShapeDtypeStruct((n_col, CAP, lanes), BF16),
            jax.ShapeDtypeStruct((n_col, CAP, col_lanes + LANES), BF16),
        ),
        in_specs=[hbm, hbm, hbm, hbm, vmem, vmem],
        out_specs=(vmem, vmem, vmem, vmem),
        scratch_shapes=[
            pltpu.VMEM((rows + 2 * DILATION_STEP, width), BF16),
            pltpu.VMEM((chunks, 3 * width, CHUNK), BF16),
            pltpu.VMEM((rows, width), BF16),
            pltpu.VMEM((bins, width), F32),
            pltpu.VMEM((slots, rows), BF16),
            pltpu.VMEM(pair_proj.shape, BF16),
            pltpu.VMEM(donor_w.shape, BF16),
            pltpu.VMEM((bins, lanes), F32),
            pltpu.VMEM((bins, lanes), F32),
            pltpu.VMEM((n_col, CAP, lanes), BF16),
            pltpu.VMEM((n_col, CAP, col_lanes + LANES), BF16),
            dma,
            dma((2,)),
            dma((chunks, 3)),
            dma((2,)),
            dma((2,)),
            dma((n_col - 1,)),
            dma((n_col - 1,)),
            dma((n_col - 1,)),
            dma((n_col - 1,)),
            dma((n_col - 1,)),
            dma((n_col - 1,)),
            dma((n_row,)),
            dma((n_row,)),
        ],
        compiler_params=pltpu.CompilerParams(
            collective_id=0, has_side_effects=True, vmem_limit_bytes=56 * 1024 * 1024
        ),
        name="trunk",
    )(
        sequence,
        filter_weight,
        pair_proj,
        donor_w,
        donor_pos.reshape(1, listed),
        acceptor_bin.reshape(1, listed),
    )
    return pl.pallas_call(
        tiles,
        out_shape=(
            jax.ShapeDtypeStruct((tile_rows, tile_cols, lanes), BF16),
            jax.ShapeDtypeStruct((slots, lanes), BF16),
        ),
        in_specs=[vmem] * 5,
        out_specs=(vmem, vmem),
        name="tiles",
    )(*arrived, pair_out)


def solution(mesh):
    placed = (P(("row", "col"), None), P(), P(), P(), P(), P(("row", "col")), P(("row", "col")))
    return jax.shard_map(
        functools.partial(local, mesh.shape["row"], mesh.shape["col"]),
        mesh=mesh,
        in_specs=placed,
        out_specs=(P("row", "col", None), P(("row", "col"), None)),
        check_vma=False,
    )
```
